512 devices in a mesh: expert: 64 (over z, y), tensor: 8 (over x, core).
Axes of the slice: x: 4, y: 8, z: 8, core: 2. Of those that a mesh axis runs over, the one named last changes fastest.
Arguments:
- tokens: bfloat16 [3072, 4096], P('expert', 'tensor'), may hold values from -6 to 6
- cotangent: bfloat16 [3072, 4096], P('expert', 'tensor'), may hold values from -6 to 6
- expert_ids: int32 [3072, 8], P('expert'), may hold values from 0 to 63, all different within a row; in each aligned block of 48 rows (0 to 47, 48 to 95, ...) at most 8 rows name the same one
- gate_values: float32 [3072, 8], P('expert'), may hold values from 0.05 to 1
- w_gate: bfloat16 [64, 768, 4096], P('expert', 'tensor'), may hold values from -0.09375 to 0.09375
- w_up: bfloat16 [64, 768, 4096], P('expert', 'tensor'), may hold values from -0.09375 to 0.09375
- w_down: bfloat16 [64, 768, 4096], P('expert', 'tensor'), may hold values from -0.21875 to 0.21875
Outputs:
- grad_tokens: bfloat16 [3072, 4096], P('expert', 'tensor')
- grad_gate: bfloat16 [64, 768, 4096], P('expert', 'tensor')
- grad_up: bfloat16 [64, 768, 4096], P('expert', 'tensor')
- grad_down: bfloat16 [64, 768, 4096], P('expert', 'tensor')
The draws below stay inside these ranges and needn't reach their ends.
Inputs may be any that keep to these rules, and one draw needn't show every extreme that they name: `expert_ids`: each row names 8 different experts. Among the 48 tokens of one index of the expert axis no expert is named more than 8 times, and in every draw some expert is named exactly 8 times there.
All inputs are finite; a program needn't handle non-finite values.
Results may differ from the reference program's by a relative error of at most 0.019.
Values may be sent and summed in bfloat16 or wider, within the bound.
No kernel may reach another device: no remote copies, remote signals or barrier semaphores. Data moves between devices by JAX's collectives and lax.ppermute only.
A program may use at most 64 MiB of HBM per device.

```python
import math
import jax
import jax.numpy as jnp
import numpy as np
from jax import lax

D = 4096
HID = 768
TOP = 8
TOK_DEV = 48
EXPERTS = 64
CAP = 8
TOKENS = 3072
N_EXPERT = 64
N_TENSOR = 8


def steps_of(rng, extent, pieces, least, high):
    gain = 1.0
    for dim, shards_of in pieces:
        heights = jax.random.uniform(jax.random.fold_in(jax.random.fold_in(rng, 6), dim), (shards_of,), jnp.float32, least / len(pieces), high / len(pieces))
        gain = gain * jnp.repeat(jnp.exp(heights), extent[dim] // shards_of).reshape((-1,) + (1,) * (len(extent) - 1 - dim))
    return gain


def shared_out(rng, own, number, rows, count, top, reach, slope):
    sequence = jax.random.permutation(rng, count)
    heavy_load, common = load_shares(count, rows * top, reach, slope, True), load_shares(count, rows * top, reach, slope, False)
    places = jnp.arange(count)

    def named(lengths, turn):
        used = int((lengths > 0).sum())
        fixed = max(1, used // 4)
        moved = fixed + (places - fixed + turn * (used - fixed)) % max(1, count - fixed)
        return jnp.zeros((count,), jnp.int32).at[sequence[jnp.where(places < fixed, places, moved)]].set(jnp.asarray(lengths, jnp.int32))

    lengths = jnp.where(number % 4 == 0, named(heavy_load, number // 4), named(common, number - number // 4 - 1))
    mixed = jax.random.permutation(jax.random.fold_in(own, 3), count)
    donor, receiver = mixed[0:count // 2 * 2:2], mixed[1:count // 2 * 2:2]
    room = jnp.minimum(lengths[donor] - 1, reach - lengths[receiver]) // 2
    room = jnp.where((donor == sequence[0]) | (receiver == sequence[0]) | (lengths[receiver] == 0), 0, jnp.maximum(room, 0))
    moved = jax.random.randint(jax.random.fold_in(own, 4), (count // 2,), 0, 1 << 20) % (room + 1)
    lengths = lengths.at[donor].add(-moved).at[receiver].add(moved)
    members = jnp.searchsorted(jnp.cumsum(lengths), jnp.arange(rows * top), side="right").astype(jnp.int32)
    listing = members.reshape(top, rows).T
    listing = listing[jax.random.permutation(jax.random.fold_in(own, 1), rows)]
    turn = jax.random.randint(jax.random.fold_in(own, 2), (rows, 1), 0, top)
    return jnp.take_along_axis(listing, (jnp.arange(top)[None, :] + turn) % top, axis=1)


def load_shares(count, total, reach, lean, full):
    loads = [(1 << 20) // math.isqrt(rank ** lean) + 1 for rank in range(1, count + 1)]
    largest = reach if full else min(reach, max(-(-total // count), total * loads[0] // sum(loads)))
    least = 1 if total - largest >= count - 1 else 0
    counts, surplus = [largest] + [least] * (count - 1), total - largest - least * (count - 1)
    while surplus > 0:
        free = [i for i in range(1, count) if counts[i] < largest] or [i for i in range(1, count) if counts[i] < reach]
        pool, remaining = sum([loads[i] for i in free]), surplus
        for i in free:
            more = min(reach - counts[i], max(1, remaining * loads[i] // pool), surplus)
            counts[i] = counts[i] + more
            surplus = surplus - more
    return np.array(counts)


def scatter_about(rng, extent, scale, bound, split=(), held_as=jnp.bfloat16):
    entries = jax.random.normal(rng, extent, jnp.float32) * scale
    if len(split) > 0:
        entries = steps_of(rng, extent, split, -0.22, 0.18) * entries
    return jnp.clip(entries, min=-bound, max=bound).astype(held_as)


def setup_inputs(seed: int = 0) -> dict:
    arg_keys = jax.random.split(jax.random.key(seed), 8)
    tokens = scatter_about(arg_keys[0], (TOKENS, D), 1.0, 6.0, ((0, 64), (1, 8)))
    cotangent = scatter_about(arg_keys[1], (TOKENS, D), 1.0, 6.0, ((0, 64), (1, 8)))
    expert_ids_keys = jax.random.split(jax.random.fold_in(arg_keys[2], 1), TOKENS // TOK_DEV)
    expert_ids_turns = jax.random.permutation(jax.random.fold_in(arg_keys[2], 3), TOKENS // TOK_DEV)
    expert_ids = jax.vmap(lambda own, number: shared_out(jax.random.fold_in(arg_keys[2], 2), own, number, TOK_DEV, EXPERTS, TOP, CAP, 2))(expert_ids_keys, expert_ids_turns).reshape((TOKENS, TOP))
    gate_values = jnp.clip(jnp.exp(math.log(1.0) - 2.9957323 * jax.random.uniform(arg_keys[3], (TOKENS, TOP), jnp.float32) ** steps_of(arg_keys[3], (TOKENS, TOP), ((0, 64),), -0.2, 0.2)), 0.05, 1.0)
    w_gate = scatter_about(arg_keys[4], (EXPERTS, HID, D), D ** -0.5, 0.09375, ((0, 64), (1, 8)))
    w_up = scatter_about(arg_keys[5], (EXPERTS, HID, D), D ** -0.5, 0.09375, ((0, 64), (1, 8)))
    w_down = scatter_about(arg_keys[6], (EXPERTS, HID, D), HID ** -0.5, 0.21875, ((0, 64), (1, 8)))
    return dict(tokens=tokens, cotangent=cotangent, expert_ids=expert_ids, gate_values=gate_values, w_gate=w_gate, w_up=w_up, w_down=w_down)


def reference(tokens, cotangent, expert_ids, gate_values, w_gate, w_up, w_down):
    per_block = TOK_DEV * TOP
    flat_ids = expert_ids.reshape(N_EXPERT, per_block)
    onehot = (flat_ids[:, :, None] == jnp.arange(EXPERTS, dtype=jnp.int32)[None, None, :]).astype(jnp.int32)
    before = jnp.cumsum(onehot, axis=1) - onehot
    slot_pos = jnp.sum(before * onehot, axis=2).astype(jnp.int32)
    token_index = (jnp.arange(TOKENS, dtype=jnp.int32)[:, None] + jnp.zeros((1, TOP), jnp.int32)).reshape(N_EXPERT, per_block)
    source = jnp.arange(N_EXPERT, dtype=jnp.int32)[:, None] + jnp.zeros((1, per_block), jnp.int32)
    slot_owner = jnp.full((EXPERTS, N_EXPERT, CAP), -1, jnp.int32).at[flat_ids, source, slot_pos].set(token_index)
    slot_gate = jnp.zeros((EXPERTS, N_EXPERT, CAP), jnp.float32).at[flat_ids, source, slot_pos].set(gate_values.reshape(N_EXPERT, per_block))
    row_count = N_EXPERT * CAP

    def one_expert(accumulated, per_expert):
        owner_e, gate_e, gate_mat, up_mat, down_mat = per_expert
        occupied = (owner_e >= 0).reshape(-1)
        row_index = jnp.maximum(owner_e, 0).reshape(-1).astype(jnp.int32)
        rows_x = jnp.where(occupied[:, None], tokens[row_index], jnp.zeros((), jnp.bfloat16))
        scaled = gate_e.reshape(-1)[:, None] * cotangent[row_index].astype(jnp.float32)
        rows_d = jnp.where(occupied[:, None], scaled, jnp.zeros((), jnp.float32)).astype(jnp.bfloat16)
        gate_pre = jnp.dot(rows_x, gate_mat.T, preferred_element_type=jnp.float32)
        up_pre = jnp.dot(rows_x, up_mat.T, preferred_element_type=jnp.float32)
        sigmoid = jax.nn.sigmoid(gate_pre)
        active = gate_pre * sigmoid
        hidden = (active * up_pre).astype(jnp.bfloat16)
        hidden_grad = jnp.dot(rows_d, down_mat.T, preferred_element_type=jnp.float32)
        up_grad = (hidden_grad * active).astype(jnp.bfloat16)
        gate_grad = (hidden_grad * up_pre * sigmoid * (1.0 + gate_pre * (1.0 - sigmoid))).astype(jnp.bfloat16)
        grad_g = jnp.dot(gate_grad.T, rows_x, preferred_element_type=jnp.float32).astype(jnp.bfloat16)
        grad_u = jnp.dot(up_grad.T, rows_x, preferred_element_type=jnp.float32).astype(jnp.bfloat16)
        grad_d = jnp.dot(hidden.T, rows_d, preferred_element_type=jnp.float32).astype(jnp.bfloat16)
        part_sums = jnp.einsum('rph,phd->prd', gate_grad.reshape(row_count, N_TENSOR, -1).astype(jnp.float32), gate_mat.reshape(N_TENSOR, -1, D).astype(jnp.float32))
        part_sums = part_sums + jnp.einsum('rph,phd->prd', up_grad.reshape(row_count, N_TENSOR, -1).astype(jnp.float32), up_mat.reshape(N_TENSOR, -1, D).astype(jnp.float32))
        rounded = lax.optimization_barrier(part_sums.astype(jnp.bfloat16))
        row_grad = jnp.sum(rounded.astype(jnp.float32), axis=0).astype(jnp.bfloat16)
        addend = jnp.where(occupied[:, None], row_grad.astype(jnp.float32), jnp.zeros((), jnp.float32))
        accumulated = accumulated.at[row_index].add(addend)
        return accumulated, (grad_g, grad_u, grad_d)

    accumulated, grads = lax.scan(one_expert, jnp.zeros((TOKENS, D), jnp.float32), (slot_owner, slot_gate, w_gate, w_up, w_down))
    return accumulated.astype(jnp.bfloat16), grads[0], grads[1], grads[2]
```

```python
import jax
import jax.numpy as jnp
from jax import lax
from jax.experimental import pallas as pl
from jax.experimental.pallas import tpu as pltpu
from jax.sharding import PartitionSpec as P

TOP = 8
CAP = 8
X_CHIPS = 4
F32, BF16 = jnp.float32, jnp.bfloat16
VMEM = pl.BlockSpec(memory_space=pltpu.VMEM)
ANY = pl.BlockSpec(memory_space=pl.ANY)


def dot(a, b, ca, cb):
    return lax.dot_general(a, b, (((ca,), (cb,)), ((), ())), preferred_element_type=F32)


def pieces(v):
    out = []
    for _ in range(3):
        part = v.astype(BF16)
        out.append(part)
        v = v - part.astype(F32)
    return out


def dispatch_kernel(ids_ref, gate_ref, tok_ref, cot_ref, wg_ref, wu_ref, wd_ref,
                    sent_ref, place_ref, m0, m1, m2, m3, sems):
    chip = lax.axis_index("tensor") // 2
    hid = wg_ref.shape[0]
    feats = wg_ref.shape[1] // X_CHIPS
    copies = []
    for s, m in enumerate((m0, m1, m2, m3)):
        start = pl.multiple_of(lax.rem(chip + s, X_CHIPS) * feats, feats)
        for j, w in enumerate((wg_ref, wu_ref, wd_ref)):
            copies.append(pltpu.make_async_copy(
                w.at[:, pl.ds(start, feats)], m.at[pl.ds(j * hid, hid), :], sems.at[s, j]))
            copies[-1].start()
    toks, width = tok_ref.shape
    slots = sent_ref.shape[0]
    experts = slots // CAP
    ids = ids_ref[...]
    gates = gate_ref[...]
    expert_iota = lax.broadcasted_iota(jnp.int32, (toks, experts), 1)
    chosen = jnp.zeros((toks, experts), F32)
    weight = jnp.zeros((toks, experts), F32)
    for k in range(TOP):
        hit = ids[:, k:k + 1] == expert_iota
        chosen = chosen + hit.astype(F32)
        weight = weight + jnp.where(hit, gates[:, k:k + 1], 0.0)
    row = lax.broadcasted_iota(jnp.int32, (toks, toks), 0)
    col = lax.broadcasted_iota(jnp.int32, (toks, toks), 1)
    earlier = (col < row).astype(F32).astype(BF16)
    chosen_b = chosen.astype(BF16)
    slot = dot(earlier, chosen_b, 1, 0)
    spread = (lax.broadcasted_iota(jnp.int32, (experts, slots), 1) // CAP
              == lax.broadcasted_iota(jnp.int32, (experts, slots), 0)).astype(F32).astype(BF16)
    chosen_s = dot(chosen_b, spread, 1, 0)
    slot_s = dot(slot.astype(BF16), spread, 1, 0)
    capacity = (lax.broadcasted_iota(jnp.int32, (toks, slots), 1) % CAP).astype(F32)
    place = jnp.where((chosen_s > 0.5) & (slot_s == capacity), 1.0, 0.0)
    place_b = place.astype(BF16)
    place_ref[...] = place_b
    sent_ref[:, :width] = dot(place_b, tok_ref[...], 0, 0).astype(BF16)
    ones = jnp.ones((toks, 128), BF16)
    scale = jnp.zeros((slots, 128), F32)
    for part in pieces(weight):
        spread_part = dot(part, spread, 1, 0) * place
        scale = scale + dot(spread_part.astype(BF16), ones, 0, 0)
    rows_d = dot(place_b, cot_ref[...], 0, 0)
    for j in range(width // 128):
        sent_ref[:, width + j * 128:width + (j + 1) * 128] = (
            scale * rows_d[:, j * 128:(j + 1) * 128]).astype(BF16)
    for c in copies:
        c.wait()


def partial_kernel(own_ref, oth_ref, m0, m1, m2, m3, p0, p1, p2, p3):
    core = lax.rem(lax.axis_index("tensor"), 2)
    width = own_ref.shape[1] // 2
    hid = m0.shape[0] // 3
    mine = pl.ds(pl.multiple_of(core * width, width), width)
    theirs = pl.ds(pl.multiple_of((1 - core) * width, width), width)
    for m, p in ((m2, p2), (m1, p1), (m3, p3), (m0, p0)):
        gu = dot(m[:2 * hid, mine], own_ref[:, :width], 1, 1)
        gu = gu + dot(m[:2 * hid, theirs], oth_ref[:, :width], 1, 1)
        p[:2 * hid, :] = gu.astype(p.dtype)
        dn = dot(m[2 * hid:, mine], own_ref[:, width:], 1, 1)
        dn = dn + dot(m[2 * hid:, theirs], oth_ref[:, width:], 1, 1)
        p[2 * hid:, :] = dn.astype(p.dtype)


def act_kernel(p0, r1, r2, r3, gu_ref, hidden_ref):
    hid = hidden_ref.shape[0]
    total = p0[...] + r1[...].astype(F32) + r2[...].astype(F32) + r3[...].astype(F32)
    gate_pre, up_pre, hidden_grad = total[:hid], total[hid:2 * hid], total[2 * hid:]
    sigmoid = jax.nn.sigmoid(gate_pre)
    active = gate_pre * sigmoid
    hidden_ref[...] = (active * up_pre).astype(BF16)
    gu_ref[hid:, :] = (hidden_grad * active).astype(BF16)
    gu_ref[:hid, :] = (hidden_grad * up_pre * sigmoid * (1.0 + gate_pre * (1.0 - sigmoid))).astype(BF16)


def row_kernel(g0, g1, g2, g3, m0, m1, m2, m3, keep_ref, send_ref):
    core = lax.rem(lax.axis_index("tensor"), 2)
    width = keep_ref.shape[1]
    two = g0.shape[0]
    mine = pl.ds(pl.multiple_of(core * width, width), width)
    theirs = pl.ds(pl.multiple_of((1 - core) * width, width), width)
    for part, out in ((theirs, send_ref), (mine, keep_ref)):
        total = None
        for g, m in ((g0, m0), (g1, m1), (g2, m2), (g3, m3)):
            term = dot(g[...], m[:two, part], 0, 0)
            total = term if total is None else total + term
        out[...] = total.astype(out.dtype)


def grad_kernel(gu_ref, hidden_ref, rows_ref, gg_ref, gup_ref, gd_ref):
    hid = hidden_ref.shape[0]
    width = gg_ref.shape[1]
    both = dot(gu_ref[...], rows_ref[0, :, :width], 1, 0)
    gg_ref[...] = both[:hid].astype(BF16)
    gup_ref[...] = both[hid:].astype(BF16)
    gd_ref[...] = dot(hidden_ref[...], rows_ref[0, :, width:], 1, 0).astype(BF16)


def combine_kernel(place_ref, arrived_ref, out_ref):
    out_ref[...] = dot(place_ref[...], arrived_ref[...], 1, 0).astype(BF16)


def call(kernel, outs, n_in, scratch=(), in_specs=None, out_specs=None, flops=0, nbytes=0):
    return pl.pallas_call(
        kernel,
        out_shape=[jax.ShapeDtypeStruct(s, d) for s, d in outs],
        in_specs=in_specs or [VMEM] * n_in,
        out_specs=out_specs or [VMEM] * len(outs),
        scratch_shapes=list(scratch),
        compiler_params=pltpu.CompilerParams(vmem_limit_bytes=40 << 20),
        cost_estimate=pl.CostEstimate(flops=flops, bytes_accessed=nbytes, transcendentals=0),
    )


def on_device(tokens, cotangent, expert_ids, gate_values, w_gate, w_up, w_down):
    toks, width = tokens.shape
    hid, feats = w_gate.shape[1], w_gate.shape[2]
    groups = lax.axis_size("expert")
    n_tensor = lax.axis_size("tensor")
    slots = groups * CAP
    chip_feats = feats // X_CHIPS
    w_gate, w_up, w_down = (w.reshape(hid, feats) for w in (w_gate, w_up, w_down))

    def shift(v, s):
        return lax.ppermute(v, "tensor", [(i, (i + 2 * s) % n_tensor) for i in range(n_tensor)])

    def sibling(v):
        return lax.ppermute(v, "tensor", [(i, i ^ 1) for i in range(n_tensor)])

    message = ((3 * hid, chip_feats), BF16)
    sent, place, *blocks = call(
        dispatch_kernel,
        [((slots, 2 * width), BF16), ((toks, slots), BF16)] + [message] * X_CHIPS,
        7,
        scratch=[pltpu.SemaphoreType.DMA((X_CHIPS, 3))],
        in_specs=[VMEM] * 4 + [ANY] * 3,
        out_specs=[VMEM] * 2 + [ANY] * X_CHIPS,
        flops=10**8, nbytes=6 << 20,
    )(expert_ids, gate_values, tokens, cotangent, w_gate, w_up, w_down)
    rows = lax.all_to_all(sent.reshape(groups, CAP, 2 * width), "expert", 0, 0, tiled=True)
    rows = rows.reshape(slots, 2 * width)
    weights = [blocks[0]] + [shift(blocks[s], s) for s in range(1, X_CHIPS)]
    every = lax.all_gather(rows, "tensor", axis=0)
    other = sibling(rows)
    parts = call(
        partial_kernel,
        [((3 * hid, slots), F32)] + [((3 * hid, slots), BF16)] * 3,
        6, flops=12 * 10**8, nbytes=6 << 20,
    )(rows, other, *weights)
    got = [shift(parts[s], -s) for s in range(1, X_CHIPS)]
    gate_up, hidden = call(
        act_kernel, [((2 * hid, slots), BF16), ((hid, slots), BF16)], 4,
        flops=10**7, nbytes=2 << 20,
    )(parts[0], *got)
    gathered = [gate_up] + [shift(gate_up, s) for s in range(1, X_CHIPS)]
    keep, send = call(
        row_kernel, [((slots, width), F32), ((slots, width), BF16)], 8,
        flops=8 * 10**8, nbytes=5 << 20,
    )(*gathered, *weights)
    row_grad = (keep + sibling(send).astype(F32)).astype(BF16)
    arrived = lax.all_to_all(row_grad.reshape(groups, CAP, width), "expert", 0, 0, tiled=True)
    grads = pl.pallas_call(
        grad_kernel,
        grid=(n_tensor,),
        out_shape=[jax.ShapeDtypeStruct((hid, feats), BF16)] * 3,
        in_specs=[
            pl.BlockSpec((2 * hid, slots), lambda q: (0, 0)),
            pl.BlockSpec((hid, slots), lambda q: (0, 0)),
            pl.BlockSpec((1, slots, 2 * width), lambda q: (q, 0, 0)),
        ],
        out_specs=[pl.BlockSpec((hid, width), lambda q: (0, q))] * 3,
        compiler_params=pltpu.CompilerParams(vmem_limit_bytes=40 << 20),
        cost_estimate=pl.CostEstimate(flops=12 * 10**8, bytes_accessed=11 << 20, transcendentals=0),
    )(gate_up, hidden, every)
    (grad_tokens,) = call(
        combine_kernel, [((toks, width), BF16)], 2, flops=10**7, nbytes=1 << 20,
    )(place, arrived.reshape(slots, width))
    return (grad_tokens, *(g.reshape(1, hid, feats) for g in grads))


def solution(mesh):
    return jax.shard_map(
        on_device,
        mesh=mesh,
        in_specs=(
            P("expert", "tensor"),
            P("expert", "tensor"),
            P("expert", None),
            P("expert", None),
            P("expert", "tensor", None),
            P("expert", "tensor", None),
            P("expert", "tensor", None),
        ),
        out_specs=(
            P("expert", "tensor"),
            P("expert", "tensor", None),
            P("expert", "tensor", None),
            P("expert", "tensor", None),
        ),
        check_vma=False,
    )
```

```python
import jax
import jax.numpy as jnp
from jax import lax
from jax.experimental import pallas as pl
from jax.experimental.pallas import tpu as pltpu
from jax.sharding import PartitionSpec as P

TOP = 8
CAP = 8
X_CHIPS = 4
F32, BF16 = jnp.float32, jnp.bfloat16
VMEM = pl.BlockSpec(memory_space=pltpu.VMEM)
ANY = pl.BlockSpec(memory_space=pl.ANY)
HBM = pl.BlockSpec(memory_space=pltpu.HBM)


def dot(a, b, ca, cb):
    return lax.dot_general(a, b, (((ca,), (cb,)), ((), ())), preferred_element_type=F32)


def dispatch_kernel(ids_ref, gate_ref, tok_ref, cot_ref, wg_ref, wu_ref, wd_ref,
                    sent_ref, place_ref, m0, m1, m2, m3, sems):
    chip = lax.axis_index("tensor") // 2
    hid = wg_ref.shape[0]
    feats = wg_ref.shape[1] // X_CHIPS
    copies = []
    for s, m in enumerate((m0, m1, m2, m3)):
        start = pl.multiple_of(lax.rem(chip + s, X_CHIPS) * feats, feats)
        for j, w in enumerate((wg_ref, wu_ref, wd_ref)):
            copies.append(pltpu.make_async_copy(
                w.at[:, pl.ds(start, feats)], m.at[pl.ds(j * hid, hid), :], sems.at[s, j]))
            copies[-1].start()
    toks, width = tok_ref.shape
    slots = sent_ref.shape[0]
    experts = slots // CAP
    ids = ids_ref[...]
    gates = gate_ref[...]
    expert_iota = lax.broadcasted_iota(jnp.int32, (experts, toks), 0)
    chosen = jnp.zeros((experts, toks), F32)
    weight = jnp.zeros((experts, toks), F32)
    for k in range(TOP):
        hit = ids[k:k + 1, :] == expert_iota
        chosen = chosen + jnp.where(hit, 1.0, 0.0)
        weight = weight + jnp.where(hit, gates[k:k + 1, :], 0.0)
    row = lax.broadcasted_iota(jnp.int32, (toks, toks), 0)
    col = lax.broadcasted_iota(jnp.int32, (toks, toks), 1)
    earlier = jnp.where(row < col, 1.0, 0.0).astype(BF16)
    slot = dot(chosen.astype(BF16), earlier, 1, 0)
    slot = jnp.where(chosen > 0.5, slot, -1.0)
    capacity = lax.broadcasted_iota(jnp.int32, (experts, CAP, toks), 1).astype(F32)
    place = jnp.where(slot[:, None, :] == capacity, 1.0, 0.0)
    scale = jnp.sum((place * weight[:, None, :]).reshape(slots, toks), axis=1, keepdims=True)
    place_b = place.reshape(slots, toks).astype(BF16)
    place_ref[...] = place_b
    sent_ref[:, :width] = dot(place_b, tok_ref[...], 1, 0).astype(BF16)
    sent_ref[:, width:] = (scale * dot(place_b, cot_ref[...], 1, 0)).astype(BF16)
    for c in copies:
        c.wait()


def partial_kernel(own_ref, oth_ref, m0, m1, m2, m3, p0, p1, p2, p3):
    core = lax.rem(lax.axis_index("tensor"), 2)
    width = own_ref.shape[1] // 2
    hid = m0.shape[0] // 3
    mine = pl.ds(pl.multiple_of(core * width, width), width)
    theirs = pl.ds(pl.multiple_of((1 - core) * width, width), width)
    for m, p in ((m2, p2), (m1, p1), (m3, p3), (m0, p0)):
        gu = dot(m[:2 * hid, mine], own_ref[:, :width], 1, 1)
        gu = gu + dot(m[:2 * hid, theirs], oth_ref[:, :width], 1, 1)
        p[:2 * hid, :] = gu.astype(p.dtype)
        dn = dot(m[2 * hid:, mine], own_ref[:, width:], 1, 1)
        dn = dn + dot(m[2 * hid:, theirs], oth_ref[:, width:], 1, 1)
        p[2 * hid:, :] = dn.astype(p.dtype)


def act_kernel(p0, r1, r2, r3, gu_ref, hidden_ref):
    hid = hidden_ref.shape[0]
    total = p0[...] + r1[...].astype(F32) + r2[...].astype(F32) + r3[...].astype(F32)
    gate_pre, up_pre, hidden_grad = total[:hid], total[hid:2 * hid], total[2 * hid:]
    sigmoid = jax.nn.sigmoid(gate_pre)
    active = gate_pre * sigmoid
    hidden_ref[...] = (active * up_pre).astype(BF16)
    gu_ref[hid:, :] = (hidden_grad * active).astype(BF16)
    gu_ref[:hid, :] = (hidden_grad * up_pre * sigmoid * (1.0 + gate_pre * (1.0 - sigmoid))).astype(BF16)


def row_kernel(g0, g1, g2, g3, m0, m1, m2, m3, keep_ref, send_ref):
    core = lax.rem(lax.axis_index("tensor"), 2)
    width = keep_ref.shape[1]
    two = g0.shape[0]
    mine = pl.ds(pl.multiple_of(core * width, width), width)
    theirs = pl.ds(pl.multiple_of((1 - core) * width, width), width)
    for part, out in ((theirs, send_ref), (mine, keep_ref)):
        total = None
        for g, m in ((g0, m0), (g1, m1), (g2, m2), (g3, m3)):
            term = dot(g[...], m[:two, part], 0, 0)
            total = term if total is None else total + term
        out[...] = total.astype(out.dtype)


def grad_kernel(gu_ref, hidden_ref, rows_ref, gg_ref, gup_ref, gd_ref):
    hid = hidden_ref.shape[0]
    width = gg_ref.shape[1]
    both = dot(gu_ref[...], rows_ref[0, :, :width], 1, 0)
    gg_ref[...] = both[:hid].astype(BF16)
    gup_ref[...] = both[hid:].astype(BF16)
    gd_ref[...] = dot(hidden_ref[...], rows_ref[0, :, width:], 1, 0).astype(BF16)


def combine_kernel(place_ref, arrived_ref, out_ref):
    out_ref[...] = dot(place_ref[...], arrived_ref[...], 0, 0).astype(BF16)


def call(kernel, outs, n_in, scratch=(), in_specs=None, out_specs=None, flops=0, nbytes=0):
    return pl.pallas_call(
        kernel,
        out_shape=[jax.ShapeDtypeStruct(s, d) for s, d in outs],
        in_specs=in_specs or [VMEM] * n_in,
        out_specs=out_specs or [VMEM] * len(outs),
        scratch_shapes=list(scratch),
        compiler_params=pltpu.CompilerParams(vmem_limit_bytes=40 << 20),
        cost_estimate=pl.CostEstimate(flops=flops, bytes_accessed=nbytes, transcendentals=0),
    )


def in_hbm(v):
    return pltpu.with_memory_space_constraint(v, pltpu.HBM)


def on_device(tokens, cotangent, expert_ids, gate_values, w_gate, w_up, w_down):
    toks, width = tokens.shape
    hid, feats = w_gate.shape[1], w_gate.shape[2]
    groups = lax.axis_size("expert")
    n_tensor = lax.axis_size("tensor")
    slots = groups * CAP
    chip_feats = feats // X_CHIPS
    w_gate, w_up, w_down = (in_hbm(w.reshape(hid, feats)) for w in (w_gate, w_up, w_down))

    def shift(v, s):
        return lax.ppermute(v, "tensor", [(i, (i + 2 * s) % n_tensor) for i in range(n_tensor)])

    def sibling(v):
        return lax.ppermute(v, "tensor", [(i, i ^ 1) for i in range(n_tensor)])

    message = ((3 * hid, chip_feats), BF16)
    sent, place, *blocks = call(
        dispatch_kernel,
        [((slots, 2 * width), BF16), ((slots, toks), BF16)] + [message] * X_CHIPS,
        7,
        scratch=[pltpu.SemaphoreType.DMA((X_CHIPS, 3))],
        in_specs=[VMEM] * 4 + [HBM] * 3,
        out_specs=[VMEM] * 2 + [ANY] * X_CHIPS,
        flops=10**8, nbytes=6 << 20,
    )(in_hbm(expert_ids.T), in_hbm(gate_values.T), in_hbm(tokens), in_hbm(cotangent), w_gate, w_up, w_down)
    rows = lax.all_to_all(sent.reshape(groups, CAP, 2 * width), "expert", 0, 0, tiled=True)
    rows = in_hbm(rows.reshape(slots, 2 * width))
    moved = {s: shift(blocks[s], s) for s in (2, 1, 3)}
    rows, *weights = lax.optimization_barrier((rows, moved[1], moved[2], moved[3]))
    weights = [blocks[0]] + weights
    every = lax.all_gather(rows, "tensor", axis=0)
    other = sibling(rows)
    parts = call(
        partial_kernel,
        [((3 * hid, slots), F32)] + [((3 * hid, slots), BF16)] * 3,
        6, flops=12 * 10**8, nbytes=6 << 20,
    )(rows, other, *weights)
    got = [shift(parts[s], -s) for s in range(1, X_CHIPS)]
    gate_up, hidden = call(
        act_kernel, [((2 * hid, slots), BF16), ((hid, slots), BF16)], 4,
        flops=10**7, nbytes=2 << 20,
    )(parts[0], *got)
    gathered = [gate_up] + [shift(gate_up, s) for s in range(1, X_CHIPS)]
    keep, send = call(
        row_kernel, [((slots, width), F32), ((slots, width), BF16)], 8,
        flops=8 * 10**8, nbytes=5 << 20,
    )(*gathered, *weights)
    row_grad = (keep + sibling(send).astype(F32)).astype(BF16)
    arrived = lax.all_to_all(row_grad.reshape(groups, CAP, width), "expert", 0, 0, tiled=True)
    grads = pl.pallas_call(
        grad_kernel,
        grid=(n_tensor,),
        out_shape=[jax.ShapeDtypeStruct((hid, feats), BF16)] * 3,
        in_specs=[
            pl.BlockSpec((2 * hid, slots), lambda q: (0, 0)),
            pl.BlockSpec((hid, slots), lambda q: (0, 0)),
            pl.BlockSpec((1, slots, 2 * width), lambda q: (q, 0, 0)),
        ],
        out_specs=[pl.BlockSpec((hid, width), lambda q: (0, q))] * 3,
        compiler_params=pltpu.CompilerParams(vmem_limit_bytes=40 << 20),
        cost_estimate=pl.CostEstimate(flops=12 * 10**8, bytes_accessed=11 << 20, transcendentals=0),
    )(gate_up, hidden, in_hbm(every))
    arrived, *grads = lax.optimization_barrier((arrived, *grads))
    (grad_tokens,) = call(
        combine_kernel, [((toks, width), BF16)], 2, flops=10**7, nbytes=1 << 20,
    )(place, arrived.reshape(slots, width))
    return (grad_tokens, *(g.reshape(1, hid, feats) for g in grads))


def solution(mesh):
    return jax.shard_map(
        on_device,
        mesh=mesh,
        in_specs=(
            P("expert", "tensor"),
            P("expert", "tensor"),
            P("expert", None),
            P("expert", None),
            P("expert", "tensor", None),
            P("expert", "tensor", None),
            P("expert", "tensor", None),
        ),
        out_specs=(
            P("expert", "tensor"),
            P("expert", "tensor", None),
            P("expert", "tensor", None),
            P("expert", "tensor", None),
        ),
        check_vma=False,
    )
```

```python
import jax
import jax.numpy as jnp
from jax import lax
from jax.experimental import pallas as pl
from jax.experimental.pallas import tpu as pltpu
from jax.sharding import PartitionSpec as P

TOP = 8
CAP = 8
X_CHIPS = 4
F32, BF16 = jnp.float32, jnp.bfloat16
VMEM = pl.BlockSpec(memory_space=pltpu.VMEM)
HBM = pl.BlockSpec(memory_space=pltpu.HBM)


def dot(a, b, ca, cb):
    return lax.dot_general(a, b, (((ca,), (cb,)), ((), ())), preferred_element_type=F32)


def halves(width):
    core = lax.rem(lax.axis_index("tensor"), 2)
    mine = pl.ds(pl.multiple_of(core * width, width), width)
    theirs = pl.ds(pl.multiple_of((1 - core) * width, width), width)
    return mine, theirs


def owner(s):
    return lax.rem(lax.axis_index("tensor") // 2 + X_CHIPS - s, X_CHIPS)


def dispatch_kernel(ids_ref, gate_ref, tok_ref, cot_ref, wg_ref, wu_ref, wd_ref,
                    sent_ref, place_ref, b0, b1, b2, b3, sems):
    hid = wg_ref.shape[0]
    feats = b0.shape[1]
    chip = lax.axis_index("tensor") // 2
    copies = []
    for s, block in enumerate((b0, b1, b2, b3)):
        start = pl.multiple_of(lax.rem(chip + s, X_CHIPS) * feats, feats)
        for j, w in enumerate((wg_ref, wu_ref, wd_ref)):
            copies.append(pltpu.make_async_copy(
                w.at[:, pl.ds(start, feats)], block.at[pl.ds(j * hid, hid), :], sems.at[s, j]))
            copies[-1].start()
    toks, width = tok_ref.shape
    slots = sent_ref.shape[0]
    experts = slots // CAP
    ids = ids_ref[...]
    gates = gate_ref[...]
    expert_iota = lax.broadcasted_iota(jnp.int32, (experts, toks), 0)
    chosen = jnp.zeros((experts, toks), F32)
    weight = jnp.zeros((experts, toks), F32)
    for k in range(TOP):
        hit = ids[k:k + 1, :] == expert_iota
        chosen = chosen + jnp.where(hit, 1.0, 0.0)
        weight = weight + jnp.where(hit, gates[k:k + 1, :], 0.0)
    row = lax.broadcasted_iota(jnp.int32, (toks, toks), 0)
    col = lax.broadcasted_iota(jnp.int32, (toks, toks), 1)
    earlier = jnp.where(row < col, 1.0, 0.0).astype(BF16)
    slot = dot(chosen.astype(BF16), earlier, 1, 0)
    slot = jnp.where(chosen > 0.5, slot, -1.0)
    capacity = lax.broadcasted_iota(jnp.int32, (experts, CAP, toks), 1).astype(F32)
    place = jnp.where(slot[:, None, :] == capacity, 1.0, 0.0)
    scale = jnp.sum((place * weight[:, None, :]).reshape(slots, toks), axis=1, keepdims=True)
    place_b = place.reshape(slots, toks).astype(BF16)
    place_ref[...] = place_b
    sent_ref[:, :width] = dot(place_b, tok_ref[...], 1, 0).astype(BF16)
    sent_ref[:, width:] = (scale * dot(place_b, cot_ref[...], 1, 0)).astype(BF16)
    for c in copies:
        c.wait()


def partial_kernel(own_ref, oth_ref, w0, w1, w2, w3, p_ref):
    width = own_ref.shape[1] // 2
    hid = w0.shape[0] // 3
    mine, theirs = halves(width)
    for s, w_ref in enumerate((w0, w1, w2, w3)):
        q = owner(s)
        gu = dot(w_ref[:2 * hid, mine], own_ref[:, :width], 1, 1)
        gu = gu + dot(w_ref[:2 * hid, theirs], oth_ref[:, :width], 1, 1)
        p_ref[q, :2 * hid, :] = gu.astype(BF16)
        dn = dot(w_ref[2 * hid:, mine], own_ref[:, width:], 1, 1)
        dn = dn + dot(w_ref[2 * hid:, theirs], oth_ref[:, width:], 1, 1)
        p_ref[q, 2 * hid:, :] = dn.astype(BF16)


def act_kernel(p_ref, out_ref):
    hid = p_ref.shape[1] // 3
    total = p_ref[0].astype(F32)
    for q in range(1, X_CHIPS):
        total = total + p_ref[q].astype(F32)
    gate_pre, up_pre, hidden_grad = total[:hid], total[hid:2 * hid], total[2 * hid:]
    sigmoid = jax.nn.sigmoid(gate_pre)
    active = gate_pre * sigmoid
    gate_grad = hidden_grad * up_pre * sigmoid * (1.0 + gate_pre * (1.0 - sigmoid))
    for q in range(X_CHIPS):
        out_ref[q, :hid, :] = gate_grad.astype(BF16)
        out_ref[q, hid:2 * hid, :] = (hidden_grad * active).astype(BF16)
        out_ref[q, 2 * hid:, :] = (active * up_pre).astype(BF16)


def row_kernel(g_ref, w0, w1, w2, w3, keep_ref, send_ref):
    width = keep_ref.shape[1]
    two = 2 * (g_ref.shape[1] // 3)
    mine, theirs = halves(width)
    for part, out in ((theirs, send_ref), (mine, keep_ref)):
        total = None
        for s, w_ref in enumerate((w0, w1, w2, w3)):
            term = dot(g_ref[owner(s), :two, :], w_ref[:two, part], 0, 0)
            total = term if total is None else total + term
        out[...] = total.astype(out.dtype)


def grad_kernel(g_ref, own_ref, oth_ref, o0, o1, o2, o3):
    width = own_ref.shape[1] // 2
    two = 2 * (g_ref.shape[1] // 3)
    mine, theirs = halves(width)
    for s, out_ref in enumerate((o0, o1, o2, o3)):
        q = owner(s)
        for cols, rows in ((mine, own_ref), (theirs, oth_ref)):
            out_ref[:two, cols] = dot(g_ref[q, :two, :], rows[:, :width], 1, 0).astype(BF16)
            out_ref[two:, cols] = dot(g_ref[q, two:, :], rows[:, width:], 1, 0).astype(BF16)


def assemble_kernel(b0, b1, b2, b3, gg_ref, gu_ref, gd_ref):
    hid = gg_ref.shape[0]
    feats = b0.shape[1]
    chip = lax.axis_index("tensor") // 2
    for s, b in enumerate((b0, b1, b2, b3)):
        cols = pl.ds(pl.multiple_of(lax.rem(chip + s, X_CHIPS) * feats, feats), feats)
        gg_ref[:, cols] = b[:hid, :]
        gu_ref[:, cols] = b[hid:2 * hid, :]
        gd_ref[:, cols] = b[2 * hid:, :]


def combine_kernel(place_ref, arrived_ref, out_ref):
    out_ref[...] = dot(place_ref[...], arrived_ref[...], 0, 0).astype(BF16)


def call(kernel, outs, n_in, scratch=(), in_specs=None, flops=0, nbytes=0):
    return pl.pallas_call(
        kernel,
        out_shape=[jax.ShapeDtypeStruct(s, d) for s, d in outs],
        in_specs=in_specs or [VMEM] * n_in,
        out_specs=[VMEM] * len(outs),
        scratch_shapes=list(scratch),
        compiler_params=pltpu.CompilerParams(vmem_limit_bytes=16 << 20),
        cost_estimate=pl.CostEstimate(flops=flops, bytes_accessed=nbytes, transcendentals=0),
    )


def in_hbm(v):
    return pltpu.with_memory_space_constraint(v, pltpu.HBM)


def on_device(tokens, cotangent, expert_ids, gate_values, w_gate, w_up, w_down):
    toks, width = tokens.shape
    hid, feats = w_gate.shape[1], w_gate.shape[2]
    groups = lax.axis_size("expert")
    n_tensor = lax.axis_size("tensor")
    slots = groups * CAP
    chip_feats = feats // X_CHIPS
    w_gate, w_up, w_down = (in_hbm(w.reshape(hid, feats)) for w in (w_gate, w_up, w_down))
    same_core = [[i for i in range(n_tensor) if i % 2 == c] for c in range(2)]

    def over_x(v):
        return lax.all_to_all(v, "tensor", 0, 0, axis_index_groups=same_core, tiled=True)

    def shift(v, s):
        return lax.ppermute(v, "tensor", [(i, (i + 2 * s) % n_tensor) for i in range(n_tensor)])

    def sibling(v):
        return lax.ppermute(v, "tensor", [(i, i ^ 1) for i in range(n_tensor)])

    wide = (3 * hid, chip_feats)
    sent, place, *blocks = call(
        dispatch_kernel,
        [((slots, 2 * width), BF16), ((slots, toks), BF16)] + [(wide, BF16)] * X_CHIPS,
        7,
        scratch=[pltpu.SemaphoreType.DMA((X_CHIPS, 3))],
        in_specs=[VMEM] * 4 + [HBM] * 3,
        flops=10**8, nbytes=6 << 20,
    )(in_hbm(expert_ids.T), in_hbm(gate_values.T), in_hbm(tokens), in_hbm(cotangent), w_gate, w_up, w_down)
    rows = lax.all_to_all(sent.reshape(groups, CAP, 2 * width), "expert", 0, 0, tiled=True)
    rows = rows.reshape(slots, 2 * width)
    got = {s: shift(blocks[s], s) for s in (2, 1, 3)}
    rows, *weights = lax.optimization_barrier((rows, got[1], got[2], got[3]))
    weights = [blocks[0]] + weights
    other = sibling(rows)
    (parts,) = call(partial_kernel, [((X_CHIPS, 3 * hid, slots), BF16)], 6, flops=12 * 10**8, nbytes=6 << 20)(rows, other, *weights)
    (acts,) = call(act_kernel, [((X_CHIPS, 3 * hid, slots), BF16)], 1, flops=10**7, nbytes=2 << 20)(over_x(parts))
    gathered = (over_x(acts),)
    keep, send = call(
        row_kernel, [((slots, width), F32), ((slots, width), BF16)], 5,
        flops=8 * 10**8, nbytes=5 << 20,
    )(*gathered, *weights)
    grads = call(grad_kernel, [(wide, BF16)] * X_CHIPS, 3, flops=12 * 10**8, nbytes=6 << 20)(*gathered, rows, other)
    row_grad = (keep + sibling(send).astype(F32)).astype(BF16)
    arrived = lax.all_to_all(row_grad.reshape(groups, CAP, width), "expert", 0, 0, tiled=True)
    got = {s: shift(grads[s], -s) for s in (2, 1, 3)}
    outs = call(assemble_kernel, [((hid, feats), BF16)] * 3, 4, nbytes=5 << 20)(grads[0], got[1], got[2], got[3])
    (grad_tokens,) = call(
        combine_kernel, [((toks, width), BF16)], 2, flops=10**7, nbytes=1 << 20,
    )(place, arrived.reshape(slots, width))
    return (grad_tokens, *(g.reshape(1, hid, feats) for g in outs))


def solution(mesh):
    return jax.shard_map(
        on_device,
        mesh=mesh,
        in_specs=(
            P("expert", "tensor"),
            P("expert", "tensor"),
            P("expert", None),
            P("expert", None),
            P("expert", "tensor", None),
            P("expert", "tensor", None),
            P("expert", "tensor", None),
        ),
        out_specs=(
            P("expert", "tensor"),
            P("expert", "tensor", None),
            P("expert", "tensor", None),
            P("expert", "tensor", None),
        ),
        check_vma=False,
    )
```

```python
import jax
import jax.numpy as jnp
from jax import lax
from jax.experimental import pallas as pl
from jax.experimental.pallas import tpu as pltpu
from jax.sharding import PartitionSpec as P

TOP = 8
CAP = 8
X_CHIPS = 4
F32, BF16 = jnp.float32, jnp.bfloat16
VMEM = pl.BlockSpec(memory_space=pltpu.VMEM)
HBM = pl.BlockSpec(memory_space=pltpu.HBM)
ANY = pl.BlockSpec(memory_space=pl.ANY)


def dot(a, b, ca, cb):
    return lax.dot_general(a, b, (((ca,), (cb,)), ((), ())), preferred_element_type=F32)


def halves(width):
    core = lax.rem(lax.axis_index("tensor"), 2)
    mine = pl.ds(pl.multiple_of(core * width, width), width)
    theirs = pl.ds(pl.multiple_of((1 - core) * width, width), width)
    return mine, theirs


def owner(s):
    return lax.rem(lax.axis_index("tensor") // 2 + X_CHIPS - s, X_CHIPS)


def dispatch_kernel(ids_ref, gate_ref, tok_ref, cot_ref, wg_ref, wu_ref, wd_ref,
                    sent_ref, place_ref, b0, b1, b2, b3, sems):
    hid = wg_ref.shape[0]
    feats = b0.shape[1]
    chip = lax.axis_index("tensor") // 2
    copies = []
    for s, block in enumerate((b0, b1, b2, b3)):
        start = pl.multiple_of(lax.rem(chip + s, X_CHIPS) * feats, feats)
        for j, w in enumerate((wg_ref, wu_ref, wd_ref)):
            copies.append(pltpu.make_async_copy(
                w.at[:, pl.ds(start, feats)], block.at[pl.ds(j * hid, hid), :], sems.at[s, j]))
            copies[-1].start()
    toks, width = tok_ref.shape
    slots = sent_ref.shape[0]
    experts = slots // CAP
    ids = ids_ref[...]
    gates = gate_ref[...]
    expert_iota = lax.broadcasted_iota(jnp.int32, (experts, toks), 0)
    chosen = jnp.zeros((experts, toks), F32)
    weight = jnp.zeros((experts, toks), F32)
    for k in range(TOP):
        hit = ids[k:k + 1, :] == expert_iota
        chosen = chosen + jnp.where(hit, 1.0, 0.0)
        weight = weight + jnp.where(hit, gates[k:k + 1, :], 0.0)
    row = lax.broadcasted_iota(jnp.int32, (toks, toks), 0)
    col = lax.broadcasted_iota(jnp.int32, (toks, toks), 1)
    earlier = jnp.where(row < col, 1.0, 0.0).astype(BF16)
    slot = dot(chosen.astype(BF16), earlier, 1, 0)
    slot = jnp.where(chosen > 0.5, slot, -1.0)
    capacity = lax.broadcasted_iota(jnp.int32, (experts, CAP, toks), 1).astype(F32)
    place = jnp.where(slot[:, None, :] == capacity, 1.0, 0.0)
    scale = jnp.sum((place * weight[:, None, :]).reshape(slots, toks), axis=1, keepdims=True)
    place_b = place.reshape(slots, toks).astype(BF16)
    place_ref[...] = place_b
    sent_ref[:, :width] = dot(place_b, tok_ref[...], 1, 0).astype(BF16)
    sent_ref[:, width:] = (scale * dot(place_b, cot_ref[...], 1, 0)).astype(BF16)
    for c in copies:
        c.wait()


def partial_kernel(own_ref, oth_ref, w0, w1, w2, w3, p_ref):
    width = own_ref.shape[1] // 2
    hid = w0.shape[0] // 3
    mine, theirs = halves(width)
    for s, w_ref in enumerate((w0, w1, w2, w3)):
        q = owner(s)
        gu = dot(w_ref[:2 * hid, mine], own_ref[:, :width], 1, 1)
        gu = gu + dot(w_ref[:2 * hid, theirs], oth_ref[:, :width], 1, 1)
        p_ref[q, :2 * hid, :] = gu.astype(BF16)
        dn = dot(w_ref[2 * hid:, mine], own_ref[:, width:], 1, 1)
        dn = dn + dot(w_ref[2 * hid:, theirs], oth_ref[:, width:], 1, 1)
        p_ref[q, 2 * hid:, :] = dn.astype(BF16)


def act_kernel(p_ref, out_ref):
    hid = p_ref.shape[1] // 3
    total = p_ref[0].astype(F32)
    for q in range(1, X_CHIPS):
        total = total + p_ref[q].astype(F32)
    gate_pre, up_pre, hidden_grad = total[:hid], total[hid:2 * hid], total[2 * hid:]
    sigmoid = jax.nn.sigmoid(gate_pre)
    active = gate_pre * sigmoid
    gate_grad = hidden_grad * up_pre * sigmoid * (1.0 + gate_pre * (1.0 - sigmoid))
    for q in range(X_CHIPS):
        out_ref[q, :hid, :] = gate_grad.astype(BF16)
        out_ref[q, hid:2 * hid, :] = (hidden_grad * active).astype(BF16)
        out_ref[q, 2 * hid:, :] = (active * up_pre).astype(BF16)


def row_kernel(g_ref, w0, w1, w2, w3, keep_ref, send_ref):
    width = keep_ref.shape[1]
    two = 2 * (g_ref.shape[1] // 3)
    mine, theirs = halves(width)
    for part, out in ((theirs, send_ref), (mine, keep_ref)):
        total = None
        for s, w_ref in enumerate((w0, w1, w2, w3)):
            term = dot(g_ref[owner(s), :two, :], w_ref[:two, part], 0, 0)
            total = term if total is None else total + term
        out[...] = total.astype(out.dtype)


def grad_kernel(g_ref, own_ref, oth_ref, kept_ref, o1, o2, o3, o0, sem):
    width = own_ref.shape[1] // 2
    two = 2 * (g_ref.shape[1] // 3)
    mine, theirs = halves(width)
    for s, out_ref in enumerate((o0, o1, o2, o3)):
        q = owner(s)
        for cols, rows in ((mine, own_ref), (theirs, oth_ref)):
            out_ref[:two, cols] = dot(g_ref[q, :two, :], rows[:, :width], 1, 0).astype(BF16)
            out_ref[two:, cols] = dot(g_ref[q, two:, :], rows[:, width:], 1, 0).astype(BF16)
        if s == 0:
            copy = pltpu.make_async_copy(o0, kept_ref, sem)
            copy.start()
    copy.wait()


def assemble_kernel(b0, b1, b2, b3, gg_ref, gu_ref, gd_ref, sems):
    hid = gg_ref.shape[0]
    feats = b0.shape[1]
    chip = lax.axis_index("tensor") // 2
    copies = []
    for s, b in enumerate((b0, b1, b2, b3)):
        start = pl.multiple_of(lax.rem(chip + s, X_CHIPS) * feats, feats)
        for j, out in enumerate((gg_ref, gu_ref, gd_ref)):
            copies.append(pltpu.make_async_copy(
                b.at[pl.ds(j * hid, hid), :], out.at[:, pl.ds(start, feats)], sems.at[s, j]))
            copies[-1].start()
    for c in copies:
        c.wait()


def combine_kernel(place_ref, arrived_ref, out_ref):
    out_ref[...] = dot(place_ref[...], arrived_ref[...], 0, 0).astype(BF16)


def call(kernel, outs, n_in, scratch=(), in_specs=None, out_specs=None, flops=0, nbytes=0):
    return pl.pallas_call(
        kernel,
        out_shape=[jax.ShapeDtypeStruct(s, d) for s, d in outs],
        in_specs=in_specs or [VMEM] * n_in,
        out_specs=out_specs or [VMEM] * len(outs),
        scratch_shapes=list(scratch),
        compiler_params=pltpu.CompilerParams(vmem_limit_bytes=16 << 20),
        cost_estimate=pl.CostEstimate(flops=flops, bytes_accessed=nbytes, transcendentals=0),
    )


def in_hbm(v):
    return pltpu.with_memory_space_constraint(v, pltpu.HBM)


def on_device(tokens, cotangent, expert_ids, gate_values, w_gate, w_up, w_down):
    toks, width = tokens.shape
    hid, feats = w_gate.shape[1], w_gate.shape[2]
    groups = lax.axis_size("expert")
    n_tensor = lax.axis_size("tensor")
    slots = groups * CAP
    chip_feats = feats // X_CHIPS
    w_gate, w_up, w_down = (in_hbm(w.reshape(hid, feats)) for w in (w_gate, w_up, w_down))
    same_core = [[i for i in range(n_tensor) if i % 2 == c] for c in range(2)]

    def over_x(v):
        return lax.all_to_all(v, "tensor", 0, 0, axis_index_groups=same_core, tiled=True)

    def shift(v, s):
        return lax.ppermute(v, "tensor", [(i, (i + 2 * s) % n_tensor) for i in range(n_tensor)])

    def sibling(v):
        return lax.ppermute(v, "tensor", [(i, i ^ 1) for i in range(n_tensor)])

    wide = (3 * hid, chip_feats)
    sent, place, *blocks = call(
        dispatch_kernel,
        [((slots, 2 * width), BF16), ((slots, toks), BF16)] + [(wide, BF16)] * X_CHIPS,
        7,
        scratch=[pltpu.SemaphoreType.DMA((X_CHIPS, 3))],
        in_specs=[VMEM] * 4 + [HBM] * 3,
        flops=10**8, nbytes=6 << 20,
    )(in_hbm(expert_ids.T), in_hbm(gate_values.T), in_hbm(tokens), in_hbm(cotangent), w_gate, w_up, w_down)
    rows = lax.all_to_all(sent.reshape(groups, CAP, 2 * width), "expert", 0, 0, tiled=True)
    rows = rows.reshape(slots, 2 * width)
    got = {s: shift(blocks[s], s) for s in (2, 1, 3)}
    rows, w2, w1, w3 = lax.optimization_barrier((rows, got[2], got[1], got[3]))
    weights = (blocks[0], w1, w2, w3)
    other = sibling(rows)
    (parts,) = call(partial_kernel, [((X_CHIPS, 3 * hid, slots), BF16)], 6, flops=12 * 10**8, nbytes=6 << 20)(rows, other, *weights)
    (acts,) = call(act_kernel, [((X_CHIPS, 3 * hid, slots), BF16)], 1, flops=10**7, nbytes=2 << 20)(over_x(parts))
    gathered = (over_x(acts),)
    grads = call(
        grad_kernel, [(wide, BF16)] * X_CHIPS, 3,
        scratch=[pltpu.VMEM(wide, BF16), pltpu.SemaphoreType.DMA(())],
        out_specs=[HBM] + [VMEM] * 3, flops=12 * 10**8, nbytes=6 << 20,
    )(*gathered, rows, other)
    gathered, *grads = lax.optimization_barrier((gathered, *grads))
    keep, send = call(
        row_kernel, [((slots, width), F32), ((slots, width), BF16)], 5,
        flops=8 * 10**8, nbytes=5 << 20,
    )(*gathered, *weights)
    row_grad = (keep + sibling(send).astype(F32)).astype(BF16)
    arrived = lax.all_to_all(row_grad.reshape(groups, CAP, width), "expert", 0, 0, tiled=True)
    got = {s: shift(grads[s], -s) for s in (2, 1, 3)}
    outs = call(
        assemble_kernel, [((hid, feats), BF16)] * 3, 4,
        scratch=[pltpu.SemaphoreType.DMA((X_CHIPS, 3))],
        in_specs=[ANY] * 4, flops=2 * 10**11, nbytes=5 << 20,
    )(grads[0], got[1], got[2], got[3])
    arrived, *outs = lax.optimization_barrier((arrived, *outs))
    (grad_tokens,) = call(
        combine_kernel, [((toks, width), BF16)], 2, flops=10**7, nbytes=1 << 20,
    )(place, arrived.reshape(slots, width))
    return (grad_tokens, *(g.reshape(1, hid, feats) for g in outs))


def solution(mesh):
    return jax.shard_map(
        on_device,
        mesh=mesh,
        in_specs=(
            P("expert", "tensor"),
            P("expert", "tensor"),
            P("expert", None),
            P("expert", None),
            P("expert", "tensor", None),
            P("expert", "tensor", None),
            P("expert", "tensor", None),
        ),
        out_specs=(
            P("expert", "tensor"),
            P("expert", "tensor", None),
            P("expert", "tensor", None),
            P("expert", "tensor", None),
        ),
        check_vma=False,
    )
```

```python
import jax
import jax.numpy as jnp
from jax import lax
from jax.experimental import pallas as pl
from jax.experimental.pallas import tpu as pltpu
from jax.sharding import PartitionSpec as P

TOP = 8
CAP = 8
X_CHIPS = 4
F32, BF16 = jnp.float32, jnp.bfloat16
VMEM = pl.BlockSpec(memory_space=pltpu.VMEM)
HBM = pl.BlockSpec(memory_space=pltpu.HBM)
ANY = pl.BlockSpec(memory_space=pl.ANY)


def dot(a, b, ca, cb):
    return lax.dot_general(a, b, (((ca,), (cb,)), ((), ())), preferred_element_type=F32)


def halves(width):
    core = lax.rem(lax.axis_index("tensor"), 2)
    mine = pl.ds(pl.multiple_of(core * width, width), width)
    theirs = pl.ds(pl.multiple_of((1 - core) * width, width), width)
    return mine, theirs


def owner(s):
    return lax.rem(lax.axis_index("tensor") // 2 + X_CHIPS - s, X_CHIPS)


def dispatch_kernel(ids_ref, gate_ref, tok_ref, cot_ref, wg_ref, wu_ref, wd_ref,
                    sent_ref, place_ref, b0, b1, b2, b3, sems):
    hid = wg_ref.shape[0]
    feats = b0.shape[1]
    chip = lax.axis_index("tensor") // 2
    copies = []
    for s, block in enumerate((b0, b1, b2, b3)):
        start = pl.multiple_of(lax.rem(chip + s, X_CHIPS) * feats, feats)
        for j, w in enumerate((wg_ref, wu_ref, wd_ref)):
            copies.append(pltpu.make_async_copy(
                w.at[:, pl.ds(start, feats)], block.at[pl.ds(j * hid, hid), :], sems.at[s, j]))
            copies[-1].start()
    toks, width = tok_ref.shape
    slots = sent_ref.shape[0]
    experts = slots // CAP
    ids = ids_ref[...]
    gates = gate_ref[...]
    expert_iota = lax.broadcasted_iota(jnp.int32, (experts, toks), 0)
    chosen = jnp.zeros((experts, toks), F32)
    weight = jnp.zeros((experts, toks), F32)
    for k in range(TOP):
        hit = ids[k:k + 1, :] == expert_iota
        chosen = chosen + jnp.where(hit, 1.0, 0.0)
        weight = weight + jnp.where(hit, gates[k:k + 1, :], 0.0)
    row = lax.broadcasted_iota(jnp.int32, (toks, toks), 0)
    col = lax.broadcasted_iota(jnp.int32, (toks, toks), 1)
    earlier = jnp.where(row < col, 1.0, 0.0).astype(BF16)
    slot = dot(chosen.astype(BF16), earlier, 1, 0)
    slot = jnp.where(chosen > 0.5, slot, -1.0)
    capacity = lax.broadcasted_iota(jnp.int32, (experts, CAP, toks), 1).astype(F32)
    place = jnp.where(slot[:, None, :] == capacity, 1.0, 0.0)
    scale = jnp.sum((place * weight[:, None, :]).reshape(slots, toks), axis=1, keepdims=True)
    place_b = place.reshape(slots, toks).astype(BF16)
    place_ref[...] = place_b
    sent_ref[:, :width] = dot(place_b, tok_ref[...], 1, 0).astype(BF16)
    sent_ref[:, width:] = (scale * dot(place_b, cot_ref[...], 1, 0)).astype(BF16)
    for c in copies:
        c.wait()


def partial_kernel(own_ref, oth_ref, w0, w1, w2, w3, p_ref):
    width = own_ref.shape[1] // 2
    hid = w0.shape[0] // 3
    mine, theirs = halves(width)
    for s, w_ref in enumerate((w0, w1, w2, w3)):
        q = owner(s)
        gu = dot(w_ref[:2 * hid, mine], own_ref[:, :width], 1, 1)
        gu = gu + dot(w_ref[:2 * hid, theirs], oth_ref[:, :width], 1, 1)
        p_ref[q, :2 * hid, :] = gu.astype(BF16)
        dn = dot(w_ref[2 * hid:, mine], own_ref[:, width:], 1, 1)
        dn = dn + dot(w_ref[2 * hid:, theirs], oth_ref[:, width:], 1, 1)
        p_ref[q, 2 * hid:, :] = dn.astype(BF16)


def act_kernel(p_ref, out_ref):
    hid = p_ref.shape[1] // 3
    total = p_ref[0].astype(F32)
    for q in range(1, X_CHIPS):
        total = total + p_ref[q].astype(F32)
    gate_pre, up_pre, hidden_grad = total[:hid], total[hid:2 * hid], total[2 * hid:]
    sigmoid = jax.nn.sigmoid(gate_pre)
    active = gate_pre * sigmoid
    gate_grad = hidden_grad * up_pre * sigmoid * (1.0 + gate_pre * (1.0 - sigmoid))
    for q in range(X_CHIPS):
        out_ref[q, :hid, :] = gate_grad.astype(BF16)
        out_ref[q, hid:2 * hid, :] = (hidden_grad * active).astype(BF16)
        out_ref[q, 2 * hid:, :] = (active * up_pre).astype(BF16)


def row_kernel(g_ref, w0, w1, w2, w3, keep_ref, send_ref):
    width = keep_ref.shape[1]
    two = 2 * (g_ref.shape[1] // 3)
    mine, theirs = halves(width)
    for part, out in ((theirs, send_ref), (mine, keep_ref)):
        total = None
        for s, w_ref in enumerate((w0, w1, w2, w3)):
            term = dot(g_ref[owner(s), :two, :], w_ref[:two, part], 0, 0)
            total = term if total is None else total + term
        out[...] = total.astype(out.dtype)


def grad_kernel(g_ref, own_ref, oth_ref, kept_ref, o1, o2, o3, o0, sem):
    width = own_ref.shape[1] // 2
    two = 2 * (g_ref.shape[1] // 3)
    mine, theirs = halves(width)
    for s, out_ref in enumerate((o0, o1, o2, o3)):
        q = owner(s)
        for cols, rows in ((mine, own_ref), (theirs, oth_ref)):
            out_ref[:two, cols] = dot(g_ref[q, :two, :], rows[:, :width], 1, 0).astype(BF16)
            out_ref[two:, cols] = dot(g_ref[q, two:, :], rows[:, width:], 1, 0).astype(BF16)
        if s == 0:
            copy = pltpu.make_async_copy(o0, kept_ref, sem)
            copy.start()
    copy.wait()


def place_columns(blocks, outs, sems):
    hid, feats = outs[0].shape[0], blocks[0][1].shape[1]
    copies = []
    for i, (s, b) in enumerate(blocks):
        chip = lax.axis_index("tensor") // 2
        start = pl.multiple_of(lax.rem(chip + s, X_CHIPS) * feats, feats)
        for j, out in enumerate(outs):
            copies.append(pltpu.make_async_copy(
                b.at[pl.ds(j * hid, hid), :], out.at[:, pl.ds(start, feats)], sems.at[i, j]))
            copies[-1].start()
    for c in copies:
        c.wait()


def first_columns_kernel(b0, b2, gg_ref, gu_ref, gd_ref, sems):
    place_columns(((0, b0), (2, b2)), (gg_ref, gu_ref, gd_ref), sems)


def last_columns_kernel(b1, b3, gg_in, gu_in, gd_in, gg_ref, gu_ref, gd_ref, sems):
    place_columns(((1, b1), (3, b3)), (gg_ref, gu_ref, gd_ref), sems)


def combine_kernel(place_ref, arrived_ref, out_ref):
    out_ref[...] = dot(place_ref[...], arrived_ref[...], 0, 0).astype(BF16)


def call(kernel, outs, n_in, scratch=(), in_specs=None, out_specs=None, aliases=None, flops=0, nbytes=0):
    return pl.pallas_call(
        kernel,
        out_shape=[o if isinstance(o, pl.MemoryRef) else jax.ShapeDtypeStruct(*o) for o in outs],
        in_specs=in_specs or [VMEM] * n_in,
        out_specs=out_specs or [VMEM] * len(outs),
        scratch_shapes=list(scratch),
        input_output_aliases=aliases or {},
        compiler_params=pltpu.CompilerParams(vmem_limit_bytes=16 << 20),
        cost_estimate=pl.CostEstimate(flops=flops, bytes_accessed=nbytes, transcendentals=0),
    )


def in_hbm(v):
    return pltpu.with_memory_space_constraint(v, pltpu.HBM)


def on_device(tokens, cotangent, expert_ids, gate_values, w_gate, w_up, w_down):
    toks, width = tokens.shape
    hid, feats = w_gate.shape[1], w_gate.shape[2]
    groups = lax.axis_size("expert")
    n_tensor = lax.axis_size("tensor")
    slots = groups * CAP
    chip_feats = feats // X_CHIPS
    w_gate, w_up, w_down = (in_hbm(w.reshape(hid, feats)) for w in (w_gate, w_up, w_down))
    same_core = [[i for i in range(n_tensor) if i % 2 == c] for c in range(2)]

    def over_x(v):
        return lax.all_to_all(v, "tensor", 0, 0, axis_index_groups=same_core, tiled=True)

    def shift(v, s):
        return lax.ppermute(v, "tensor", [(i, (i + 2 * s) % n_tensor) for i in range(n_tensor)])

    def sibling(v):
        return lax.ppermute(v, "tensor", [(i, i ^ 1) for i in range(n_tensor)])

    wide = (3 * hid, chip_feats)
    sent, place, *blocks = call(
        dispatch_kernel,
        [((slots, 2 * width), BF16), ((slots, toks), BF16)] + [pltpu.HBM(wide, BF16)] * X_CHIPS,
        7,
        scratch=[pltpu.SemaphoreType.DMA((X_CHIPS, 3))],
        in_specs=[VMEM] * 4 + [HBM] * 3,
        flops=10**8, nbytes=6 << 20,
    )(in_hbm(expert_ids.T), in_hbm(gate_values.T), in_hbm(tokens), in_hbm(cotangent), w_gate, w_up, w_down)
    rows = lax.all_to_all(sent.reshape(groups, CAP, 2 * width), "expert", 0, 0, tiled=True)
    rows = rows.reshape(slots, 2 * width)
    got = {s: shift(blocks[s], s) for s in (2, 1, 3)}
    rows, w2, w1, w3 = lax.optimization_barrier((rows, got[2], got[1], got[3]))
    weights = (blocks[0], w1, w2, w3)
    other = sibling(rows)
    (parts,) = call(partial_kernel, [((X_CHIPS, 3 * hid, slots), BF16)], 6, flops=12 * 10**8, nbytes=6 << 20)(rows, other, *weights)
    (acts,) = call(act_kernel, [((X_CHIPS, 3 * hid, slots), BF16)], 1, flops=10**7, nbytes=2 << 20)(over_x(parts))
    gathered = (over_x(acts),)
    grads = call(
        grad_kernel, [pltpu.HBM(wide, BF16)] * X_CHIPS, 3,
        scratch=[pltpu.VMEM(wide, BF16), pltpu.SemaphoreType.DMA(())],
        out_specs=[HBM] + [VMEM] * 3, flops=12 * 10**8, nbytes=6 << 20,
    )(*gathered, rows, other)
    gathered, *grads = lax.optimization_barrier((gathered, *grads))
    keep, send = call(
        row_kernel, [((slots, width), F32), ((slots, width), BF16)], 5,
        flops=8 * 10**8, nbytes=5 << 20,
    )(*gathered, *weights)
    row_grad = (keep + sibling(send).astype(F32)).astype(BF16)
    arrived = lax.all_to_all(row_grad.reshape(groups, CAP, width), "expert", 0, 0, tiled=True)
    got = {s: shift(grads[s], -s) for s in (2, 1, 3)}
    whole = [pltpu.HBM((hid, feats), BF16)] * 3
    outs = call(
        first_columns_kernel, whole, 2,
        scratch=[pltpu.SemaphoreType.DMA((2, 3))],
        out_specs=[HBM] * 3, flops=10**10, nbytes=2 << 20,
    )(grads[0], got[2])
    (grad_tokens,) = call(
        combine_kernel, [((toks, width), BF16)], 2, flops=10**7, nbytes=1 << 20,
    )(place, arrived.reshape(slots, width))
    near, grad_tokens = lax.optimization_barrier((got[1], grad_tokens))
    outs = call(
        last_columns_kernel, whole, 5,
        scratch=[pltpu.SemaphoreType.DMA((2, 3))],
        in_specs=[VMEM] * 2 + [HBM] * 3, out_specs=[HBM] * 3,
        aliases={2: 0, 3: 1, 4: 2}, nbytes=2 << 20,
    )(near, got[3], *outs)
    return (grad_tokens, *(g.reshape(1, hid, feats) for g in outs))


def solution(mesh):
    return jax.shard_map(
        on_device,
        mesh=mesh,
        in_specs=(
            P("expert", "tensor"),
            P("expert", "tensor"),
            P("expert", None),
            P("expert", None),
            P("expert", "tensor", None),
            P("expert", "tensor", None),
            P("expert", "tensor", None),
        ),
        out_specs=(
            P("expert", "tensor"),
            P("expert", "tensor", None),
            P("expert", "tensor", None),
            P("expert", "tensor", None),
        ),
        check_vma=False,
    )
```

```python
import jax
import jax.numpy as jnp
from jax import lax
from jax.experimental import pallas as pl
from jax.experimental.pallas import tpu as pltpu
from jax.sharding import PartitionSpec as P

TOP = 8
CAP = 8
X_CHIPS = 4
F32, BF16 = jnp.float32, jnp.bfloat16
VMEM = pl.BlockSpec(memory_space=pltpu.VMEM)
HBM = pl.BlockSpec(memory_space=pltpu.HBM)
ANY = pl.BlockSpec(memory_space=pl.ANY)


def dot(a, b, ca, cb):
    return lax.dot_general(a, b, (((ca,), (cb,)), ((), ())), preferred_element_type=F32)


def halves(width):
    core = lax.rem(lax.axis_index("tensor"), 2)
    mine = pl.ds(pl.multiple_of(core * width, width), width)
    theirs = pl.ds(pl.multiple_of((1 - core) * width, width), width)
    return mine, theirs


def owner(s):
    return lax.rem(lax.axis_index("tensor") // 2 + X_CHIPS - s, X_CHIPS)


def dispatch_kernel(ids_ref, gate_ref, tok_ref, cot_ref, wg_ref, wu_ref, wd_ref,
                    sent_ref, place_ref, b0, b1, b2, b3, sems):
    hid = wg_ref.shape[0]
    feats = b0.shape[1]
    chip = lax.axis_index("tensor") // 2
    copies = []
    for s, block in enumerate((b0, b1, b2, b3)):
        start = pl.multiple_of(lax.rem(chip + s, X_CHIPS) * feats, feats)
        for j, w in enumerate((wg_ref, wu_ref, wd_ref)):
            copies.append(pltpu.make_async_copy(
                w.at[:, pl.ds(start, feats)], block.at[pl.ds(j * hid, hid), :], sems.at[s, j]))
            copies[-1].start()
    toks, width = tok_ref.shape
    slots = sent_ref.shape[0]
    experts = slots // CAP
    ids = ids_ref[...]
    gates = gate_ref[...]
    expert_iota = lax.broadcasted_iota(jnp.int32, (experts, toks), 0)
    chosen = jnp.zeros((experts, toks), F32)
    weight = jnp.zeros((experts, toks), F32)
    for k in range(TOP):
        hit = ids[k:k + 1, :] == expert_iota
        chosen = chosen + jnp.where(hit, 1.0, 0.0)
        weight = weight + jnp.where(hit, gates[k:k + 1, :], 0.0)
    row = lax.broadcasted_iota(jnp.int32, (toks, toks), 0)
    col = lax.broadcasted_iota(jnp.int32, (toks, toks), 1)
    earlier = jnp.where(row < col, 1.0, 0.0).astype(BF16)
    slot = dot(chosen.astype(BF16), earlier, 1, 0)
    slot = jnp.where(chosen > 0.5, slot, -1.0)
    capacity = lax.broadcasted_iota(jnp.int32, (experts, CAP, toks), 1).astype(F32)
    place = jnp.where(slot[:, None, :] == capacity, 1.0, 0.0)
    scale = jnp.sum((place * weight[:, None, :]).reshape(slots, toks), axis=1, keepdims=True)
    place_b = place.reshape(slots, toks).astype(BF16)
    place_ref[...] = place_b
    sent_ref[:, :width] = dot(place_b, tok_ref[...], 1, 0).astype(BF16)
    sent_ref[:, width:] = (scale * dot(place_b, cot_ref[...], 1, 0)).astype(BF16)
    for c in copies:
        c.wait()


def partial_kernel(own_ref, oth_ref, w0, w1, w2, w3, p_ref):
    width = own_ref.shape[1] // 2
    hid = w0.shape[0] // 3
    mine, theirs = halves(width)
    for s, w_ref in enumerate((w0, w1, w2, w3)):
        q = owner(s)
        gu = dot(w_ref[:2 * hid, mine], own_ref[:, :width], 1, 1)
        gu = gu + dot(w_ref[:2 * hid, theirs], oth_ref[:, :width], 1, 1)
        p_ref[q, :2 * hid, :] = gu.astype(BF16)
        dn = dot(w_ref[2 * hid:, mine], own_ref[:, width:], 1, 1)
        dn = dn + dot(w_ref[2 * hid:, theirs], oth_ref[:, width:], 1, 1)
        p_ref[q, 2 * hid:, :] = dn.astype(BF16)


def act_kernel(p_ref, out_ref):
    hid = p_ref.shape[1] // 3
    total = p_ref[0].astype(F32)
    for q in range(1, X_CHIPS):
        total = total + p_ref[q].astype(F32)
    gate_pre, up_pre, hidden_grad = total[:hid], total[hid:2 * hid], total[2 * hid:]
    sigmoid = jax.nn.sigmoid(gate_pre)
    active = gate_pre * sigmoid
    gate_grad = hidden_grad * up_pre * sigmoid * (1.0 + gate_pre * (1.0 - sigmoid))
    for q in range(X_CHIPS):
        out_ref[q, :hid, :] = gate_grad.astype(BF16)
        out_ref[q, hid:2 * hid, :] = (hidden_grad * active).astype(BF16)
        out_ref[q, 2 * hid:, :] = (active * up_pre).astype(BF16)


def row_kernel(g_ref, w0, w1, w2, w3, keep_ref, send_ref):
    width = keep_ref.shape[1]
    two = 2 * (g_ref.shape[1] // 3)
    mine, theirs = halves(width)
    for part, out in ((theirs, send_ref), (mine, keep_ref)):
        total = None
        for s, w_ref in enumerate((w0, w1, w2, w3)):
            term = dot(g_ref[owner(s), :two, :], w_ref[:two, part], 0, 0)
            total = term if total is None else total + term
        out[...] = total.astype(out.dtype)


def grad_kernel(g_ref, own_ref, oth_ref, kept_ref, o1, o2, o3, o0, sem):
    width = own_ref.shape[1] // 2
    two = 2 * (g_ref.shape[1] // 3)
    mine, theirs = halves(width)
    for s, out_ref in enumerate((o0, o1, o2, o3)):
        q = owner(s)
        for cols, rows in ((mine, own_ref), (theirs, oth_ref)):
            out_ref[:two, cols] = dot(g_ref[q, :two, :], rows[:, :width], 1, 0).astype(BF16)
            out_ref[two:, cols] = dot(g_ref[q, two:, :], rows[:, width:], 1, 0).astype(BF16)
        if s == 0:
            copy = pltpu.make_async_copy(o0, kept_ref, sem)
            copy.start()
    copy.wait()


def place_columns(blocks, outs, sems):
    hid, feats = outs[0].shape[0], blocks[0][1].shape[1]
    copies = []
    for i, (s, b) in enumerate(blocks):
        chip = lax.axis_index("tensor") // 2
        start = pl.multiple_of(lax.rem(chip + s, X_CHIPS) * feats, feats)
        for j, out in enumerate(outs):
            copies.append(pltpu.make_async_copy(
                b.at[pl.ds(j * hid, hid), :], out.at[:, pl.ds(start, feats)], sems.at[i, j]))
            copies[-1].start()
    for c in copies:
        c.wait()


def first_columns_kernel(b2, b3, gg_ref, gu_ref, gd_ref, sems):
    place_columns(((2, b2), (3, b3)), (gg_ref, gu_ref, gd_ref), sems)


def last_columns_kernel(b0, b1, gg_in, gu_in, gd_in, gg_ref, gu_ref, gd_ref, sems):
    place_columns(((0, b0), (1, b1)), (gg_ref, gu_ref, gd_ref), sems)


def combine_kernel(place_ref, arrived_ref, out_ref):
    out_ref[...] = dot(place_ref[...], arrived_ref[...], 0, 0).astype(BF16)


def call(kernel, outs, n_in, scratch=(), in_specs=None, out_specs=None, aliases=None, flops=0, nbytes=0):
    return pl.pallas_call(
        kernel,
        out_shape=[o if isinstance(o, pl.MemoryRef) else jax.ShapeDtypeStruct(*o) for o in outs],
        in_specs=in_specs or [VMEM] * n_in,
        out_specs=out_specs or [VMEM] * len(outs),
        scratch_shapes=list(scratch),
        input_output_aliases=aliases or {},
        compiler_params=pltpu.CompilerParams(vmem_limit_bytes=16 << 20),
        cost_estimate=pl.CostEstimate(flops=flops, bytes_accessed=nbytes, transcendentals=0),
    )


def in_hbm(v):
    return pltpu.with_memory_space_constraint(v, pltpu.HBM)


def on_device(tokens, cotangent, expert_ids, gate_values, w_gate, w_up, w_down):
    toks, width = tokens.shape
    hid, feats = w_gate.shape[1], w_gate.shape[2]
    groups = lax.axis_size("expert")
    n_tensor = lax.axis_size("tensor")
    slots = groups * CAP
    chip_feats = feats // X_CHIPS
    w_gate, w_up, w_down = (in_hbm(w.reshape(hid, feats)) for w in (w_gate, w_up, w_down))
    same_core = [[i for i in range(n_tensor) if i % 2 == c] for c in range(2)]

    def over_x(v):
        return lax.all_to_all(v, "tensor", 0, 0, axis_index_groups=same_core, tiled=True)

    def shift(v, s):
        return lax.ppermute(v, "tensor", [(i, (i + 2 * s) % n_tensor) for i in range(n_tensor)])

    def sibling(v):
        return lax.ppermute(v, "tensor", [(i, i ^ 1) for i in range(n_tensor)])

    wide = (3 * hid, chip_feats)
    sent, place, *blocks = call(
        dispatch_kernel,
        [((slots, 2 * width), BF16), ((slots, toks), BF16)] + [pltpu.HBM(wide, BF16)] * X_CHIPS,
        7,
        scratch=[pltpu.SemaphoreType.DMA((X_CHIPS, 3))],
        in_specs=[VMEM] * 4 + [HBM] * 3,
        flops=10**8, nbytes=6 << 20,
    )(in_hbm(expert_ids.T), in_hbm(gate_values.T), in_hbm(tokens), in_hbm(cotangent), w_gate, w_up, w_down)
    rows = lax.all_to_all(sent.reshape(groups, CAP, 2 * width), "expert", 0, 0, tiled=True)
    rows = rows.reshape(slots, 2 * width)
    got = {s: shift(blocks[s], s) for s in (2, 1, 3)}
    rows, w2, w1, w3 = lax.optimization_barrier((rows, got[2], got[1], got[3]))
    weights = (blocks[0], w1, w2, w3)
    other = sibling(rows)
    (parts,) = call(partial_kernel, [((X_CHIPS, 3 * hid, slots), BF16)], 6, flops=12 * 10**8, nbytes=6 << 20)(rows, other, *weights)
    (acts,) = call(act_kernel, [((X_CHIPS, 3 * hid, slots), BF16)], 1, flops=10**7, nbytes=2 << 20)(over_x(parts))
    gathered = (over_x(acts),)
    grads = call(
        grad_kernel, [pltpu.HBM(wide, BF16)] * X_CHIPS, 3,
        scratch=[pltpu.VMEM(wide, BF16), pltpu.SemaphoreType.DMA(())],
        out_specs=[HBM] + [VMEM] * 3, flops=12 * 10**8, nbytes=6 << 20,
    )(*gathered, rows, other)
    gathered, *grads = lax.optimization_barrier((gathered, *grads))
    keep, send = call(
        row_kernel, [((slots, width), F32), ((slots, width), BF16)], 5,
        flops=8 * 10**8, nbytes=5 << 20,
    )(*gathered, *weights)
    row_grad = (keep + sibling(send).astype(F32)).astype(BF16)
    arrived = lax.all_to_all(row_grad.reshape(groups, CAP, width), "expert", 0, 0, tiled=True)
    got = {s: shift(grads[s], -s) for s in (2, 1, 3)}
    whole = [pltpu.HBM((hid, feats), BF16)] * 3
    outs = call(
        first_columns_kernel, whole, 2,
        scratch=[pltpu.SemaphoreType.DMA((2, 3))],
        out_specs=[HBM] * 3, flops=10**10, nbytes=2 << 20,
    )(got[2], got[3])
    (grad_tokens,) = call(
        combine_kernel, [((toks, width), BF16)], 2, flops=10**7, nbytes=1 << 20,
    )(place, arrived.reshape(slots, width))
    near, grad_tokens = lax.optimization_barrier((got[1], grad_tokens))
    outs = call(
        last_columns_kernel, whole, 5,
        scratch=[pltpu.SemaphoreType.DMA((2, 3))],
        in_specs=[VMEM] * 2 + [HBM] * 3, out_specs=[HBM] * 3,
        aliases={2: 0, 3: 1, 4: 2}, nbytes=2 << 20,
    )(grads[0], near, *outs)
    return (grad_tokens, *(g.reshape(1, hid, feats) for g in outs))


def solution(mesh):
    return jax.shard_map(
        on_device,
        mesh=mesh,
        in_specs=(
            P("expert", "tensor"),
            P("expert", "tensor"),
            P("expert", None),
            P("expert", None),
            P("expert", "tensor", None),
            P("expert", "tensor", None),
            P("expert", "tensor", None),
        ),
        out_specs=(
            P("expert", "tensor"),
            P("expert", "tensor", None),
            P("expert", "tensor", None),
            P("expert", "tensor", None),
        ),
        check_vma=False,
    )
```
